128 devices in a mesh: ctx: 32 (over z, y, core), mp: 4 (over x).
Axes of the slice: x: 4, y: 4, z: 4, core: 2. Of those that a mesh axis runs over, the one named last changes fastest.
Arguments:
- queries: bfloat16 [32768, 4096], P('ctx', 'mp'), may hold values from -6 to 6
- encodings: bfloat16 [256, 64, 896], P('ctx'), may hold values from -6 to 6
- key_weight: bfloat16 [896, 4096], P(None, 'mp'), may hold values from -0.1875 to 0.1875
- value_weight: bfloat16 [896, 4096], P(None, 'mp'), may hold values from -0.1875 to 0.1875
- out_grad: bfloat16 [32768, 4096], P('ctx', 'mp'), may hold values from -6 to 6
- owner_ids: int32 [512, 2], P('ctx'), may hold values from 0 to 31, all different within a row; in each aligned block of 16 rows (0 to 15, 16 to 31, ...) at most 2 rows name the same one
- block_ids: int32 [512, 2], P('ctx'), may hold values from 0 to 7
Outputs:
- retrieval_out: bfloat16 [32768, 4096], P('ctx', 'mp')
- query_grad: bfloat16 [32768, 4096], P('ctx', 'mp')
- code_grad: float32 [256, 64, 896], P('ctx', 'mp')
- key_weight_grad: float32 [896, 4096], P(None, 'mp')
- value_weight_grad: float32 [896, 4096], P(None, 'mp')
The draws below stay inside these ranges and needn't reach their ends.
Inputs may be any that keep to these rules, and one draw needn't show every extreme that they name: `owner_ids`: the 2 neighbours of a span lie with different owners; among the 16 spans of one index of ctx, no owner is named by more than 2 neighbours, a bound that some block reaches.
All inputs are finite; a program needn't handle non-finite values.
Results may differ from the reference program's by a relative error of at most 0.015.
Values may be sent and summed in bfloat16 or wider, within the bound.
No kernel may reach another device: no remote copies, remote signals or barrier semaphores. Data moves between devices by JAX's collectives and lax.ppermute only.
A program may use at most 192 MiB of HBM per device.

```python
import math
import jax
import jax.numpy as jnp
import numpy as np
from jax import lax

HEADS = 32
HD = 128
E = 896
SPAN = 64
NBRS = 2
NBR_LEN = 64
CAP = 2
TOK_DEV = 1024
BLK_DEV = 8
HQ = 4096
TOKENS = 32768
SPANS = 512
SPAN_DEV = 16
BLOCKS = 256
OWNERS = 32
N_CTX = 32


def set_ends(entries, key, low, largest):
    extent = entries.shape
    place = [jax.random.randint(jax.random.fold_in(key, axis), (), 0, extent[axis]) for axis in range(len(extent))]
    entries = entries.at[tuple(place)].set(low)
    longest = extent.index(max(extent))
    place[longest] = (place[longest] + 1) % extent[longest]
    return entries.at[tuple(place)].set(largest)


def shard_levels(rng, extent, split, smallest, largest):
    gain = 1.0
    for axis_at, shards_of in split:
        steps = jax.random.uniform(jax.random.fold_in(jax.random.fold_in(rng, 6), axis_at), (shards_of,), jnp.float32, smallest / len(split), largest / len(split))
        gain = gain * jnp.repeat(jnp.exp(steps), extent[axis_at] // shards_of).reshape((-1,) + (1,) * (len(extent) - 1 - axis_at))
    return gain


def shared_out(key, own, number, rows, count, top, most, skew):
    ranking = jax.random.permutation(key, count)
    crowded, ordinary = load_shares(count, rows * top, most, skew, True), load_shares(count, rows * top, most, skew, False)
    places = jnp.arange(count)

    def named(lengths, offset_by):
        used = int((lengths > 0).sum())
        fixed = max(1, used // 4)
        passed = fixed + (places - fixed + offset_by * (used - fixed)) % max(1, count - fixed)
        return jnp.zeros((count,), jnp.int32).at[ranking[jnp.where(places < fixed, places, passed)]].set(jnp.asarray(lengths, jnp.int32))

    lengths = jnp.where(number % 4 == 0, named(crowded, number // 4), named(ordinary, number - number // 4 - 1))
    mixed = jax.random.permutation(jax.random.fold_in(own, 3), count)
    source_of, receiver = mixed[0:count // 2 * 2:2], mixed[1:count // 2 * 2:2]
    room = jnp.minimum(lengths[source_of] - 1, most - lengths[receiver]) // 2
    room = jnp.where((source_of == ranking[0]) | (receiver == ranking[0]) | (lengths[receiver] == 0), 0, jnp.maximum(room, 0))
    passed = jax.random.randint(jax.random.fold_in(own, 4), (count // 2,), 0, 1 << 20) % (room + 1)
    lengths = lengths.at[source_of].add(-passed).at[receiver].add(passed)
    items = jnp.searchsorted(jnp.cumsum(lengths), jnp.arange(rows * top), side="right").astype(jnp.int32)
    table = items.reshape(top, rows).T
    table = table[jax.random.permutation(jax.random.fold_in(own, 1), rows)]
    offset_by = jax.random.randint(jax.random.fold_in(own, 2), (rows, 1), 0, top)
    return jnp.take_along_axis(table, (jnp.arange(top)[None, :] + offset_by) % top, axis=1)


def load_shares(count, total, reach, lean, full):
    loads = [(1 << 20) // math.isqrt(grade ** lean) + 1 for grade in range(1, count + 1)]
    largest = reach if full else min(reach, max(-(-total // count), total * loads[0] // sum(loads)))
    least = 1 if total - largest >= count - 1 else 0
    holding, rest = [largest] + [least] * (count - 1), total - largest - least * (count - 1)
    while rest > 0:
        candidates = [i for i in range(1, count) if holding[i] < largest] or [i for i in range(1, count) if holding[i] < reach]
        pool, budget = sum([loads[i] for i in candidates]), rest
        for i in candidates:
            addition = min(reach - holding[i], max(1, budget * loads[i] // pool), rest)
            holding[i] = holding[i] + addition
            rest = rest - addition
    return np.array(holding)


def bell_draw(own_key, extent, deviation, bound, cuts=(), kind=jnp.bfloat16):
    values = jax.random.normal(own_key, extent, jnp.float32) * deviation
    if len(cuts) > 0:
        values = shard_levels(own_key, extent, cuts, -0.22, 0.18) * values
    return jnp.clip(values, min=-bound, max=bound).astype(kind)


def setup_inputs(seed: int = 0) -> dict:
    seeds = jax.random.split(jax.random.key(seed), 8)
    queries = bell_draw(seeds[0], (TOKENS, HQ), 1.0, 6.0, ((0, 32), (1, 4)))
    encodings = bell_draw(seeds[1], (BLOCKS, NBR_LEN, E), 1.0, 6.0, ((0, 32),))
    key_weight = bell_draw(seeds[2], (E, HQ), E ** -0.5, 0.1875, ((1, 4),))
    value_weight = bell_draw(seeds[3], (E, HQ), E ** -0.5, 0.1875, ((1, 4),))
    out_grad = bell_draw(seeds[4], (TOKENS, HQ), 1.0, 6.0, ((0, 32), (1, 4)))
    owner_ids_keys = jax.random.split(jax.random.fold_in(seeds[5], 1), SPANS // SPAN_DEV)
    owner_ids_turns = jax.random.permutation(jax.random.fold_in(seeds[5], 3), SPANS // SPAN_DEV)
    owner_ids = jax.vmap(lambda own, number: shared_out(jax.random.fold_in(seeds[5], 2), own, number, SPAN_DEV, OWNERS, NBRS, CAP, 2))(owner_ids_keys, owner_ids_turns).reshape((SPANS, NBRS))
    block_ids = set_ends(jax.random.randint(seeds[6], (SPANS, NBRS), 0, BLK_DEV), jax.random.fold_in(seeds[6], 1), 0, BLK_DEV - 1).astype(jnp.int32)
    return {"queries": queries, "encodings": encodings, "key_weight": key_weight, "value_weight": value_weight, "out_grad": out_grad, "owner_ids": owner_ids, "block_ids": block_ids}


def rounded(values_in):
    return lax.optimization_barrier(values_in.astype(jnp.bfloat16)).astype(jnp.float32)

def reference(queries, encodings, key_weight, value_weight, out_grad, owner_ids, block_ids):
    score_scale = 1.0 / math.sqrt(HD)
    global_ids = (owner_ids * BLK_DEV + block_ids).astype(jnp.int32)
    key_wide = key_weight.astype(jnp.float32)
    value_wide = value_weight.astype(jnp.float32)
    group_queries = queries.reshape(N_CTX, TOK_DEV, HQ)
    group_grads = out_grad.reshape(N_CTX, TOK_DEV, HQ)
    group_ids = global_ids.reshape(N_CTX, SPAN_DEV * NBRS)

    def group_step(totals, inputs):
        key_total, value_total = totals
        query_rows, grad_rows, request_ids = inputs
        fetched = encodings[request_ids]
        flat_codes = fetched.reshape(SPAN_DEV * NBRS * NBR_LEN, E).astype(jnp.float32)
        key_rows = rounded(jnp.dot(flat_codes, key_wide, preferred_element_type=jnp.float32))
        value_rows = rounded(jnp.dot(flat_codes, value_wide, preferred_element_type=jnp.float32))
        key_blocks = key_rows.reshape(SPAN_DEV, NBRS * NBR_LEN, HEADS, HD)
        value_blocks = value_rows.reshape(SPAN_DEV, NBRS * NBR_LEN, HEADS, HD)
        query_blocks = query_rows.reshape(SPAN_DEV, SPAN, HEADS, HD).astype(jnp.float32)
        grad_blocks = grad_rows.reshape(SPAN_DEV, SPAN, HEADS, HD).astype(jnp.float32)
        scores = jnp.einsum('cthd,crhd->chtr', query_blocks, key_blocks, preferred_element_type=jnp.float32) * score_scale
        exponent = jnp.exp(scores)
        probability = exponent / lax.optimization_barrier(jnp.sum(exponent, axis=-1, keepdims=True))
        prob_low = rounded(probability)
        attended = jnp.einsum('chtr,crhd->cthd', prob_low, value_blocks, preferred_element_type=jnp.float32)
        attended = attended.reshape(TOK_DEV, HQ).astype(jnp.bfloat16)
        prob_grad = jnp.einsum('cthd,crhd->chtr', grad_blocks, value_blocks, preferred_element_type=jnp.float32)
        inner_sum = lax.optimization_barrier(jnp.sum(probability * prob_grad, axis=-1, keepdims=True))
        score_grad = rounded(probability * (prob_grad - inner_sum) * score_scale)
        query_grad = jnp.einsum('chtr,crhd->cthd', score_grad, key_blocks, preferred_element_type=jnp.float32)
        query_grad = query_grad.reshape(TOK_DEV, HQ).astype(jnp.bfloat16)
        key_grad = rounded(jnp.einsum('chtr,cthd->crhd', score_grad, query_blocks, preferred_element_type=jnp.float32))
        value_grad = rounded(jnp.einsum('chtr,cthd->crhd', prob_low, grad_blocks, preferred_element_type=jnp.float32))
        key_flat = key_grad.reshape(SPAN_DEV * NBRS * NBR_LEN, HQ)
        value_flat = value_grad.reshape(SPAN_DEV * NBRS * NBR_LEN, HQ)
        key_total = key_total + jnp.einsum('re,rh->eh', flat_codes, key_flat, preferred_element_type=jnp.float32)
        value_total = value_total + jnp.einsum('re,rh->eh', flat_codes, value_flat, preferred_element_type=jnp.float32)
        code_part = jnp.einsum('rh,eh->re', key_flat, key_wide, preferred_element_type=jnp.float32)
        code_part = code_part + jnp.einsum('rh,eh->re', value_flat, value_wide, preferred_element_type=jnp.float32)
        code_part = code_part.astype(jnp.bfloat16).reshape(SPAN_DEV * NBRS, NBR_LEN, E)
        return ((key_total, value_total), (attended, query_grad, code_part))
    start_totals = (jnp.zeros((E, HQ), jnp.float32), jnp.zeros((E, HQ), jnp.float32))
    totals, stacked = lax.scan(group_step, start_totals, (group_queries, group_grads, group_ids))
    attended, query_grad, code_parts = stacked
    code_grad = jax.ops.segment_sum(code_parts.reshape(N_CTX * SPAN_DEV * NBRS, NBR_LEN, E).astype(jnp.float32), global_ids.reshape(-1), num_segments=BLOCKS)
    return (attended.reshape(TOKENS, HQ), query_grad.reshape(TOKENS, HQ), code_grad, totals[0], totals[1])
```

```python
import functools
import math

import jax
import jax.numpy as jnp
from jax import lax
from jax.experimental import pallas as pl
from jax.experimental.pallas import tpu as pltpu
from jax.sharding import PartitionSpec as P

HD = 128
SPAN = 64
RING = 4
GROUP = 4
BF = jnp.bfloat16
F32 = jnp.float32

VM = pl.BlockSpec(memory_space=pltpu.VMEM)
SM = pl.BlockSpec(memory_space=pltpu.SMEM)


def from_z(x, d):
    n = RING * RING * 2
    return lax.ppermute(x, "ctx", [(s, (s - d * RING * 2) % n) for s in range(n)])


def from_y(x, d):
    pairs = []
    for s in range(RING * RING * 2):
        z, y, c = s // (2 * RING), s // 2 % RING, s % 2
        pairs.append((s, (z * RING + (y - d) % RING) * 2 + c))
    return lax.ppermute(x, "ctx", pairs)


def from_sibling(x):
    return lax.ppermute(x, "ctx", [(s, s ^ 1) for s in range(RING * RING * 2)])


def from_x(x, d):
    return lax.ppermute(x, "mp", [(s, (s - d) % RING) for s in range(RING)])


def shape(*dims, dtype=BF):
    return jax.ShapeDtypeStruct(dims, dtype)


def params(mib=48):
    return pltpu.CompilerParams(vmem_limit_bytes=mib << 20)


def select_kernel(rows, codes_ref, place_ref, *refs):
    sources, mine_ref, other_ref = refs[:8], refs[8], refs[9]
    z, y, core = place_ref[0], place_ref[1], place_ref[2]
    count = codes_ref.shape[0] // 2
    for part, out_ref in ((0, mine_ref), (1, other_ref)):

        def one(i, carry, part=part, out_ref=out_ref):
            code = codes_ref[part * count + i]
            owner, block = code // 8, code % 8
            dz = (owner // (2 * RING) - z + RING) % RING
            dy = (owner // 2 % RING - y + RING) % RING
            low = block < 4
            held = owner % 2 == core
            which = jnp.where(low, dz, RING + dy)
            index = jnp.where(low, dy * 4 + block, dz * 4 + block - 4)
            at = pl.ds(pl.multiple_of(i * rows, rows), rows)
            from_at = pl.ds(pl.multiple_of(index * rows, rows), rows)

            @pl.when(jnp.logical_not(held))
            def _():
                out_ref[at, :] = jnp.zeros((rows, out_ref.shape[1]), BF)

            for k in range(8):

                @pl.when(held & (which == k))
                def _(k=k):
                    out_ref[at, :] = sources[k][from_at, :]

            return carry

        lax.fori_loop(0, count, one, 0)


def select(codes, place, sources, rows):
    width = sources[0].shape[1]
    count = codes.shape[0] // 2
    return pl.pallas_call(
        functools.partial(select_kernel, rows),
        out_shape=(shape(count * rows, width), shape(count * rows, width)),
        in_specs=[SM, SM] + [VM] * 8,
        out_specs=(VM, VM),
        compiler_params=params(),
        cost_estimate=pl.CostEstimate(flops=0, bytes_accessed=6 << 20, transcendentals=0),
        name="select",
    )(codes, place, *sources)


def chunk_kernel(heads, aliased, *refs):
    pieces, (q_ref, g_ref, wk_ref, wv_ref) = refs[:8], refs[8:12]
    refs = refs[12 + aliased :]
    o_ref, dq_ref, own_ref, right_ref, left_ref, r2_ref, l2_ref, dkv_ref, ft_ref = refs[:9]
    fbuf, kbuf, vbuf = refs[9:]
    step = pl.program_id(0)
    part = fbuf.shape[0] // RING
    scale = 1.0 / math.sqrt(HD)
    sub = part // GROUP
    for which in range(2):

        @pl.when(step == which)
        def _(which=which):
            for d in range(RING):
                fbuf[d * part : (d + 1) * part, :] = pieces[2 * d + which][...]

    flat = fbuf[...]
    kbuf[...] = jnp.dot(flat, wk_ref[...], preferred_element_type=F32).astype(BF)
    vbuf[...] = jnp.dot(flat, wv_ref[...], preferred_element_type=F32).astype(BF)
    ft_ref[...] = flat.T
    last = (((1,), (1,)), ((), ()))
    first = (((0,), (0,)), ((), ()))

    def span(s, carry):
        tok = pl.ds(pl.multiple_of(s * SPAN, SPAN), SPAN)
        spots = [pl.ds(pl.multiple_of(d * part + s * sub, sub), sub) for d in range(RING)]
        for h in range(heads):
            cols = slice(h * HD, (h + 1) * HD)
            key = jnp.concatenate([kbuf[at, cols] for at in spots], axis=0)
            value = jnp.concatenate([vbuf[at, cols] for at in spots], axis=0)
            query = q_ref[tok, cols]
            grad = g_ref[tok, cols]
            scores = lax.dot_general(query, key, last, preferred_element_type=F32) * scale
            exponent = jnp.exp(scores)
            prob = exponent / jnp.sum(exponent, axis=-1, keepdims=True)
            low = prob.astype(BF)
            o_ref[tok, cols] = jnp.dot(low, value, preferred_element_type=F32).astype(BF)
            prob_grad = lax.dot_general(grad, value, last, preferred_element_type=F32)
            inner = jnp.sum(prob * prob_grad, axis=-1, keepdims=True)
            score_grad = (prob * (prob_grad - inner) * scale).astype(BF)
            dq_ref[tok, cols] = jnp.dot(score_grad, key, preferred_element_type=F32).astype(BF)
            dk = lax.dot_general(score_grad, query, first, preferred_element_type=F32).astype(BF)
            dv = lax.dot_general(low, grad, first, preferred_element_type=F32).astype(BF)
            for d in range(RING):
                dkv_ref[0, spots[d], cols] = dk[d * sub : (d + 1) * sub]
                dkv_ref[1, spots[d], cols] = dv[d * sub : (d + 1) * sub]
        return carry

    lax.fori_loop(0, GROUP, span, 0)
    code = lax.dot_general(dkv_ref[0], wk_ref[...], last, preferred_element_type=F32)
    code = code + lax.dot_general(dkv_ref[1], wv_ref[...], last, preferred_element_type=F32)
    code = code.astype(BF)
    rows = [code[d * part : (d + 1) * part] for d in range(RING)]
    own_ref[...] = rows[0]

    @pl.when(step == 0)
    def _():
        right_ref[...] = rows[2]
        left_ref[...] = rows[3]
        r2_ref[...] = rows[1]

    @pl.when(step == 1)
    def _():
        right_ref[...] = rows[1]
        left_ref[...] = rows[2]
        l2_ref[...] = rows[3]


def chunk(number, pieces, queries, out_grad, key_weight, value_weight, earlier):
    tok_rows, local_width = queries.shape
    part, width = pieces[0].shape
    full = part * RING
    tok = GROUP * SPAN
    whole = lambda i: (0, 0)
    at_step = lambda i: (i, 0)
    tok_spec = pl.BlockSpec((tok, local_width), lambda i: (2 * number + i, 0))
    out_shape = (
        shape(tok_rows, local_width),
        shape(tok_rows, local_width),
        shape(2 * part, width),
        shape(2 * part, width),
        shape(2 * part, width),
        shape(part, width),
        shape(part, width),
        shape(2, 2 * full, local_width),
        shape(width, 2 * full),
    )
    out_specs = (
        tok_spec,
        tok_spec,
        pl.BlockSpec((part, width), at_step),
        pl.BlockSpec((part, width), at_step),
        pl.BlockSpec((part, width), at_step),
        pl.BlockSpec((part, width), whole),
        pl.BlockSpec((part, width), whole),
        pl.BlockSpec((2, full, local_width), lambda i: (0, i, 0)),
        pl.BlockSpec((width, full), lambda i: (0, i)),
    )
    weight_spec = pl.BlockSpec((width, local_width), whole, pipeline_mode=pl.Buffered(1))
    in_specs = [pl.BlockSpec((part, width), whole)] * 8 + [
        tok_spec,
        tok_spec,
        weight_spec,
        weight_spec,
    ]
    in_specs += [pl.BlockSpec(memory_space=pl.ANY)] * len(earlier)
    flops = 2 * 2 * full * width * local_width * 4 + 2 * 6 * 2 * tok * 128 * local_width
    return pl.pallas_call(
        functools.partial(chunk_kernel, local_width // HD, len(earlier)),
        grid=(2,),
        out_shape=out_shape,
        in_specs=in_specs,
        out_specs=out_specs,
        scratch_shapes=[
            pltpu.VMEM((full, width), BF),
            pltpu.VMEM((full, local_width), BF),
            pltpu.VMEM((full, local_width), BF),
        ],
        input_output_aliases={12 + i: i for i in range(len(earlier))},
        compiler_params=params(56),
        cost_estimate=pl.CostEstimate(
            flops=flops, bytes_accessed=18 << 20, transcendentals=2 * tok * local_width
        ),
        name="attend",
    )(*pieces, queries, out_grad, key_weight, value_weight, *earlier)


def weight_kernel(which_ref, ft0, ft1, d0, d1, out_ref):
    acc = jnp.dot(ft0[...], d0[0], preferred_element_type=F32)
    acc = acc + jnp.dot(ft1[...], d1[0], preferred_element_type=F32)
    out_ref[...] = acc.astype(out_ref.dtype)


def weight_part(which, fts, dkvs, dtype):
    width, rows = fts[0].shape
    local_width = dkvs[0].shape[2]
    tile = 256
    ft_spec = pl.BlockSpec((width, rows), lambda n, w: (0, 0), pipeline_mode=pl.Buffered(1))
    d_spec = pl.BlockSpec((1, rows, tile), lambda n, w: (w[0], 0, n))
    return pl.pallas_call(
        weight_kernel,
        grid_spec=pltpu.PrefetchScalarGridSpec(
            num_scalar_prefetch=1,
            grid=(local_width // tile,),
            in_specs=[ft_spec, ft_spec, d_spec, d_spec],
            out_specs=pl.BlockSpec((width, tile), lambda n, w: (0, n)),
        ),
        out_shape=shape(width, local_width, dtype=dtype),
        compiler_params=params(),
        cost_estimate=pl.CostEstimate(
            flops=4 * rows * width * local_width, bytes_accessed=10 << 20, transcendentals=0
        ),
        name="weight_part",
    )(which, *fts, *dkvs)


def route_kernel(place_ref, own_ref, came_ref, *outs):
    group = outs[0].shape[0]
    for half in range(2):
        me = place_ref[1 - half]
        for d in range(RING):
            start = half * RING * group + (me + d) % RING * group
            at = pl.ds(pl.multiple_of(start, 16), group)
            total = own_ref[at, :].astype(F32) + came_ref[at, :].astype(F32)
            outs[half * RING + d][...] = total.astype(BF)


def route(place, own, came):
    width, local_width = own.shape
    group = width // (2 * RING)
    return pl.pallas_call(
        route_kernel,
        out_shape=(shape(group, local_width),) * 8,
        in_specs=[SM, VM, VM],
        out_specs=(VM,) * 8,
        compiler_params=params(),
        cost_estimate=pl.CostEstimate(flops=0, bytes_accessed=6 << 20, transcendentals=0),
        name="route",
    )(place, own, came)


def join_kernel(place_ref, *refs):
    pieces, out_ref = refs[:8], refs[8]
    group = pieces[0].shape[0]
    for half in range(2):
        me = place_ref[1 - half]
        for d in range(RING):
            start = half * RING * group + (me + d) % RING * group
            out_ref[pl.ds(pl.multiple_of(start, 16), group), :] = pieces[half * RING + d][...]


def join(place, pieces):
    group, local_width = pieces[0].shape
    return pl.pallas_call(
        join_kernel,
        out_shape=shape(8 * group, local_width),
        in_specs=[SM] + [VM] * 8,
        out_specs=VM,
        compiler_params=params(),
        cost_estimate=pl.CostEstimate(flops=0, bytes_accessed=4 << 20, transcendentals=0),
        name="join",
    )(place, *pieces)


def four_sum(pieces):
    a, b, c, d = [piece.astype(F32) for piece in pieces]
    return ((a + c) + (b + d)).astype(BF)


def reduce_weights(core, place, fts, dkvs):
    other = weight_part((1 - core)[None], fts, dkvs, BF)
    came = from_sibling(other)
    own = weight_part(core[None], fts, dkvs, F32)
    pieces = route(place, own, came)
    a, b = pieces[:4], pieces[4:]
    a = four_sum([a[0]] + [from_y(a[d], RING - d) for d in range(1, RING)])
    b = four_sum([b[0]] + [from_z(b[d], RING - d) for d in range(1, RING)])
    a = four_sum([a] + [from_z(a, d) for d in range(1, RING)])
    b = four_sum([b] + [from_y(b, d) for d in range(1, RING)])
    a = [a] + [from_y(a, d) for d in range(1, RING)]
    b = [b] + [from_z(b, d) for d in range(1, RING)]
    mine = join(place, a + b)
    theirs = from_sibling(mine)
    return (
        jnp.where(core == 0, mine, theirs).astype(F32),
        jnp.where(core == 0, theirs, mine).astype(F32),
    )


def slots_kernel(rows, owner_ref, *refs):
    chunks, out_ref, total, counts = (refs[:5], refs[5:10]), refs[10], refs[11], refs[12]
    part = total.shape[0] // 4
    for number, (own, right, left, second_r, second_l) in enumerate(chunks):
        base = 2 * number * part
        low = own[0:part, :].astype(F32) + left[0:part, :].astype(F32)
        low = low + second_r[...].astype(F32)
        high = own[part : 2 * part, :].astype(F32) + right[part : 2 * part, :].astype(F32)
        high = high + second_l[...].astype(F32)
        total[base : base + part, :] = low.astype(BF)
        total[base + part : base + 2 * part, :] = high.astype(BF)
    out_ref[...] = jnp.zeros_like(out_ref)
    count = owner_ref.shape[0]

    def clear(i, carry):
        counts[i] = 0
        return carry

    lax.fori_loop(0, counts.shape[0], clear, 0)

    def one(i, carry):
        owner = owner_ref[i]
        rank = counts[owner]
        counts[owner] = rank + 1
        to = pl.ds(pl.multiple_of((owner * 2 + rank) * rows, rows), rows)
        out_ref[to, :] = total[pl.ds(pl.multiple_of(i * rows, rows), rows), :]
        return carry

    lax.fori_loop(0, count, one, 0)


def to_slots(owner_flat, sums, rows, owners):
    width = sums[0].shape[1]
    count = owner_flat.shape[0]
    return pl.pallas_call(
        functools.partial(slots_kernel, rows),
        out_shape=shape(owners * 2 * rows, width),
        in_specs=[SM] + [VM] * 10,
        out_specs=VM,
        scratch_shapes=[pltpu.VMEM((count * rows, width), BF), pltpu.SMEM((owners,), jnp.int32)],
        compiler_params=params(),
        cost_estimate=pl.CostEstimate(flops=0, bytes_accessed=6 << 20, transcendentals=0),
        name="to_slots",
    )(owner_flat, *sums)


def owner_kernel(rows, place_ref, asked_ref, came_ref, out_ref):
    out_ref[...] = jnp.zeros_like(out_ref)
    z, y, core = place_ref[0], place_ref[1], place_ref[2]

    def one(asker, carry):
        dz = (asker // (2 * RING) - z + RING) % RING
        dy = (asker // 2 % RING - y + RING) % RING
        dc = (asker + core) % 2
        row = (dz * RING + dy) * 2 + dc
        for k in range(2):
            block = asked_ref[row * 2 + k]
            at = pl.ds(pl.multiple_of((asker * 2 + k) * rows, rows), rows)
            out_ref[block] += came_ref[at, :].astype(F32)
        return carry

    lax.fori_loop(0, RING * RING * 2, one, 0)


def to_owner(place, asked, came, blocks, rows):
    width = came.shape[1]
    return pl.pallas_call(
        functools.partial(owner_kernel, rows),
        out_shape=shape(blocks, rows, width, dtype=F32),
        in_specs=[SM, SM, VM],
        out_specs=VM,
        compiler_params=params(),
        cost_estimate=pl.CostEstimate(flops=0, bytes_accessed=3 << 20, transcendentals=0),
        name="to_owner",
    )(place, asked, came)


def asked_blocks(table, me):
    owner, block = table // 8, table % 8
    match = owner == me
    order = lax.broadcasted_iota(jnp.int32, table.shape, 1)
    low = jnp.min(jnp.where(match, order, 1000), axis=1, keepdims=True)
    high = jnp.max(jnp.where(match, order, -1), axis=1, keepdims=True)
    first = jnp.sum(jnp.where(match & (order == low), block, 0), axis=1)
    second = jnp.sum(jnp.where(match & (order == high), block, 0), axis=1)
    return jnp.stack([first, second], axis=1).reshape(-1)


def local(queries, encodings, key_weight, value_weight, out_grad, owner_ids, block_ids):
    block_count, block_rows, width = encodings.shape
    rows = block_rows // RING
    owners = lax.axis_size("ctx")
    me = lax.axis_index("ctx")
    core = me % 2
    place = jnp.stack([me // (2 * RING), me // 2 % RING, core]).astype(jnp.int32)
    owner_flat = owner_ids.reshape(-1)
    codes = owner_flat * block_count + block_ids.reshape(-1)
    requests = codes.shape[0]

    own = lax.dynamic_slice_in_dim(encodings, lax.axis_index("mp") * rows, rows, axis=1)
    half = block_count // 2 * rows
    a = own[: block_count // 2].reshape(half, width)
    b = own[block_count // 2 :].reshape(half, width)
    a = jnp.concatenate([a] + [from_y(a, d) for d in range(1, RING)])
    b = jnp.concatenate([b] + [from_z(b, d) for d in range(1, RING)])
    pair = jnp.stack([codes, from_sibling(codes)])
    a = [a] + [from_z(a, d) for d in range(1, RING)]
    b = [b] + [from_y(b, d) for d in range(1, RING)]
    line = jnp.stack([pair] + [from_y(pair, d) for d in range(1, RING)])
    table = jnp.stack([line] + [from_z(line, d) for d in range(1, RING)])
    asked = asked_blocks(table.reshape(owners, requests), me)
    kept, passed = select(pair.reshape(-1), place, a + b, rows)
    fetched = kept + from_sibling(passed)
    part = requests * rows // 4
    quarters = [fetched[i * part : (i + 1) * part] for i in range(4)]

    earlier, sums, fts, dkvs = (), [], [], []
    for number in range(2):
        p = quarters[2 * number : 2 * number + 2]
        ahead = [from_x(piece, 1) for piece in p]
        behind = [from_x(piece, RING - 1) for piece in p]
        far = [from_x(ahead[0], 1), from_x(behind[1], RING - 1)]
        pieces = p + ahead + far + behind
        out = chunk(number, pieces, queries, out_grad, key_weight, value_weight, earlier)
        earlier = out[:2]
        own_code, right, left, second_r, second_l, dkv, ft = out[2:]
        right = from_x(right, RING - 1)
        left = from_x(left, 1)
        second_r = from_x(second_r + right[:part], RING - 1)
        second_l = from_x(second_l + left[part:], 1)
        sums += [own_code, right, left, second_r, second_l]
        fts.append(ft)
        dkvs.append(dkv)

    slots = to_slots(owner_flat, sums, rows, owners)
    came = lax.all_to_all(
        slots.reshape(owners, 2 * rows, width), "ctx", split_axis=0, concat_axis=0, tiled=True
    )
    code_grad = to_owner(place, asked, came.reshape(owners * 2 * rows, width), block_count, rows)
    key_weight_grad, value_weight_grad = reduce_weights(core, place, fts, dkvs)
    return (earlier[0], earlier[1], code_grad, key_weight_grad, value_weight_grad)


def solution(mesh):
    placed = (
        P("ctx", "mp"),
        P("ctx", None, None),
        P(None, "mp"),
        P(None, "mp"),
        P("ctx", "mp"),
        P("ctx", None),
        P("ctx", None),
    )
    return jax.shard_map(
        local,
        mesh=mesh,
        in_specs=placed,
        out_specs=(
            P("ctx", "mp"),
            P("ctx", "mp"),
            P("ctx", "mp", None),
            P(None, "mp"),
            P(None, "mp"),
        ),
        check_vma=False,
    )
```
